32 devices in a mesh: row: 8 (over z, x), col: 4 (over y, core).
Axes of the slice: x: 2, y: 2, z: 4, core: 2. Of those that a mesh axis runs over, the one named last changes fastest.
Arguments:
- diagonal_inverses: bfloat16 [24, 2048, 2048], P('row', 'col'), may hold values from -0.125 to 0.125
- column_basis: bfloat16 [24, 2048, 256], P('row', 'col'), may hold values from -6 to 6
- row_basis: bfloat16 [24, 2048, 256], P('row', 'col'), may hold values from -0.125 to 0.125
- transfer: float32 [24, 256, 256], P('row', 'col'), may hold values from -0.375 to 0.375
- coupling: float32 [24, 256, 256], P('row', 'col'), may hold values from -6 to 6
- ranks: int32 [24], P('row'), may hold values from 128 to 256, as said below
Outputs:
- merged: float32 [24, 256, 256], P('row', 'col')
- parent_skeleton: float32 [24, 256, 256], P('row', 'col')
The draws below stay inside these ranges and needn't reach their ends.
Inputs may be any that keep to these rules, and one draw needn't show every extreme that they name: `ranks`: each rank is 128 or 256; both occur in every draw.
All inputs are finite; a program needn't handle non-finite values.
Results may differ from the reference program's by a relative error of at most 0.0021.
Values may be sent and summed in bfloat16 or wider, within the bound.
A program may use at most 64 MiB of HBM per device.

```python
import jax
import jax.numpy as jnp
from jax import lax

M = 2048
R = 256
NODE_DEV = 3
BIT = 2
NODES = 24


def draw_ranks(key, part):
    picked = jax.random.randint(key, (NODES,), 1, 3)
    picked = picked.at[0].set(2).at[1].set(1)
    return (picked * (R // 2)).astype(jnp.int32)


def block_levels(key, extent, shards, smallest, top_value):
    def one(axis_at, shards_of):
        steps = jax.random.uniform(jax.random.fold_in(jax.random.fold_in(key, 6), axis_at), (shards_of,), jnp.float32, smallest / len(shards), top_value / len(shards))
        return jnp.repeat(jnp.exp(steps), extent[axis_at] // shards_of).reshape((-1,) + (1,) * (len(extent) - axis_at - 1))

    loudness = one(*shards[0])
    for cut in shards[1:]:
        loudness = loudness * one(*cut)
    return loudness


def normal_values(key, shape, width, most, split=(), kind=jnp.bfloat16):
    values = jax.random.normal(key, shape, jnp.float32) * width
    if len(split) > 0:
        values = block_levels(key, shape, split, -0.22, 0.18) * values
    return jnp.clip(values, min=-most, max=most).astype(kind)


def setup_inputs(seed: int = 0) -> dict:
    keys = jax.random.split(jax.random.key(seed), 7)
    return {
        "diagonal_inverses": normal_values(keys[0], (NODES, M, M), M ** -0.5, 0.125, ((0, 8), (1, 4))),
        "column_basis": normal_values(keys[1], (NODES, M, R), 1.0, 6.0, ((0, 8), (1, 4))),
        "row_basis": normal_values(keys[2], (NODES, M, R), M ** -0.5, 0.125, ((0, 8), (1, 4))),
        "transfer": normal_values(keys[3], (NODES, R, R), R ** -0.5, 0.375, ((0, 8), (1, 4)), jnp.float32),
        "coupling": normal_values(keys[4], (NODES, R, R), 1.0, 6.0, ((0, 8), (1, 4)), jnp.float32),
        "ranks": draw_ranks(jax.random.fold_in(keys[6], 71), 0),
    }


def leaf_skeleton(items):
    block_entry, left_factor_basis, right_factor_basis, live_cols = items
    left_factor_basis = jnp.where(live_cols[None, :], left_factor_basis, jnp.zeros_like(left_factor_basis))
    right_factor_basis = jnp.where(live_cols[None, :], right_factor_basis, jnp.zeros_like(right_factor_basis))
    eliminated_part = jnp.dot(block_entry, left_factor_basis, preferred_element_type=jnp.float32).astype(jnp.bfloat16)
    return jnp.dot(right_factor_basis.T, eliminated_part, preferred_element_type=jnp.float32)


def reference(diagonal_inverses, column_basis, row_basis, transfer, coupling, ranks):
    node_count = transfer.shape[0]
    rank_width = transfer.shape[1]
    live_cols = jnp.arange(rank_width, dtype=jnp.int32)[None, :] < ranks[:, None]
    skeleton = lax.map(leaf_skeleton, (diagonal_inverses, column_basis, row_basis, live_cols))
    masked = transfer * live_cols[:, :, None].astype(jnp.float32)
    node_ids = jnp.arange(node_count, dtype=jnp.int32)
    sibling = jnp.bitwise_xor(node_ids // NODE_DEV, 2 ** BIT) * NODE_DEV + node_ids % NODE_DEV
    masked_sib = masked[sibling]
    highest = lax.Precision.HIGHEST
    merged = jnp.einsum('nij,njk->nik', skeleton, masked, precision=highest)
    merged = merged + jnp.einsum('nij,njk->nik', coupling, masked_sib, precision=highest)
    parent = jnp.einsum('nji,njk->nik', masked, merged, precision=highest)
    parent = parent + jnp.einsum('nji,njk->nik', masked_sib, merged[sibling], precision=highest)
    return merged, parent
```

```python
import jax
import jax.numpy as jnp
from jax import lax
from jax.experimental import pallas as pl
from jax.experimental.pallas import tpu as pltpu
from jax.sharding import PartitionSpec as P

BIT = 2
MESH = pl.DeviceIdType.MESH
LC, TY, TC, TF, TZ, TG, ZC, ZG, SC, SY, PC, PY, PZ, PD = range(14)
KINDS = 14
PIECES = 4


def kernel(
    ranks_ref, d_ref, l_ref, r_ref, t_ref, k_ref, out_ref,
    dv, lv, rv, tv, kv, tb, zb, rt, mt, xb, sbuf, sgot, ysend, ygot, pbuf, pgot,
    own_send, over_send, yin, zin, din, mv, pv,
    send_sem, recv_sem, ly_send, ly_recv, lf_send, lf_recv, d_sem, loc_sem, out_sem,
):
    nodes, block, _ = l_ref.shape
    part = t_ref.shape[1]
    width = t_ref.shape[2]
    f32, bf16 = jnp.float32, jnp.bfloat16
    c = lax.axis_index("col")
    r = lax.axis_index("row")
    core = lax.rem(c, 2)
    y = lax.div(c, 2)
    cp = c + 1 - 2 * core
    yp = c + 2 - 4 * y
    dg = cp + yp - c
    high = lax.rem(lax.div(r, 1 << BIT), 2)
    sib = r + (1 << BIT) - (2 << BIT) * high
    other = 1 - y
    last = nodes - 1

    to_core = {"col": cp}
    to_y = {"col": yp}
    to_z = {"row": sib}
    to_d = {"row": sib, "col": yp}
    slots = (c, cp, yp, dg)

    barrier = pltpu.get_barrier_semaphore()
    for device in (to_z, to_d, to_y, to_core):
        pl.semaphore_signal(barrier, inc=1, device_id=device, device_id_type=MESH)

    t_in = pltpu.make_async_copy(t_ref, tv, loc_sem.at[0])
    t_in.start()
    l_in, d_in = [], []
    for n in range(nodes):
        one = pltpu.make_async_copy(l_ref.at[n], lv.at[n, pl.ds(0, block)], d_sem.at[n, 4])
        one.start()
        l_in.append(one)
        for s in range(4):
            src = d_ref.at[n, :, pl.ds(pl.multiple_of(slots[s] * block, block), block)]
            one = pltpu.make_async_copy(src, dv.at[n, :, pl.ds(s * block, block)], d_sem.at[n, s])
            one.start()
            d_in.append(one)
        if n == 0:
            r_in = pltpu.make_async_copy(r_ref, rv, loc_sem.at[1])
            r_in.start()
    k_in = pltpu.make_async_copy(k_ref, kv, loc_sem.at[2])
    k_in.start()

    sent = []

    def remote(sems, src, dst, device):
        return pltpu.make_async_remote_copy(
            src_ref=src, dst_ref=dst, send_sem=sems[0], recv_sem=sems[1],
            device_id=device, device_id_type=MESH,
        )

    def of(kind, n):
        return send_sem.at[kind, n], recv_sem.at[kind, n]

    def send(kind, n, src, dst, device):
        one = remote(of(kind, n), src, dst, device)
        one.start()
        sent.append(one)

    def got(kind, n, ref, device):
        remote(of(kind, n), ref, ref, device).wait_recv()

    def halves(x):
        top = x.astype(bf16)
        return top, (x - top.astype(f32)).astype(bf16)

    def square(buf, n, level):
        return buf[n, :, level].reshape(width, width)

    def times_full(x, buf, n):
        top, low = halves(x)
        lhs = jnp.concatenate([top, low, top], axis=1)
        b_top, b_low = square(buf, n, 0), square(buf, n, 1)
        rhs = jnp.concatenate([b_top, b_top, b_low], axis=0)
        return jnp.dot(lhs, rhs, preferred_element_type=f32)

    def cuts(n):
        half, quarter = block // 2, block // 4
        if n < last:
            return ((0, half), (half, block - half))
        return ((0, half), (half, quarter), (half + quarter, block - half - quarter))

    def piece(n, s, cut):
        return lv.at[n, pl.ds(s * block + cut[0], cut[1])]

    def send_basis(n):
        for i, cut in enumerate(cuts(n)):
            one = remote(
                (ly_send.at[n, i], ly_recv.at[n, i]),
                l_ref.at[n, pl.ds(cut[0], cut[1])], piece(n, 2, cut), to_y,
            )
            one.start()
            sent.append(one)

    def send_core(n):
        send(LC, n, l_ref.at[n], lv.at[n, pl.ds(block, block)], to_core)

    row_at = lax.broadcasted_iota(jnp.int32, (part, width), 0) + c * part
    col_at = lax.broadcasted_iota(jnp.int32, (part, width), 1)
    zeros = jnp.zeros((part, width), bf16)

    pl.semaphore_wait(barrier, 4)
    send_basis(0)
    send_core(0)
    t_in.wait()
    for n in range(nodes):
        top, low = halves(jnp.where(row_at < ranks_ref[n], tv[n], 0.0))
        tb[n, c, 0] = top
        tb[n, c, 1] = low
        for buf in (tb, zb):
            for strip in (yp, dg):
                buf[n, strip, 1] = zeros
    for n in range(nodes):
        send(TZ, n, tb.at[n, c], zb.at[n, c], to_z)
        send(TY, n, tb.at[n, c, 0], tb.at[n, c, 0], to_y)
        send(TC, n, tb.at[n, c], tb.at[n, c], to_core)
    for n in range(1, nodes):
        send_basis(n)
        send_core(n)

    def times(n, first, size):
        span = pl.ds(first, size)
        return jnp.dot(dv[n, :, span], lv[n, span, :], preferred_element_type=f32)

    def begin(n):
        l_in[n].wait()
        for s in range(4):
            d_in[4 * n + s].wait()
        got(LC, n, lv.at[n, pl.ds(block, block)], to_core)
        return times(n, 0, 2 * block)

    def eliminate(n, total):
        before = None
        for i, cut in enumerate(cuts(n)):
            mine = piece(n, 2, cut)
            remote((ly_send.at[n, i], ly_recv.at[n, i]), mine, mine, to_y).wait_recv()
            one = remote((lf_send.at[n, i], lf_recv.at[n, i]), mine, piece(n, 3, cut), to_core)
            one.start()
            sent.append(one)
            total = total + times(n, 2 * block + cut[0], cut[1])
            theirs = piece(n, 3, cut)
            remote((lf_send.at[n, i], lf_recv.at[n, i]), theirs, theirs, to_core).wait_recv()
            total = total + times(n, 3 * block + cut[0], cut[1])
        return total

    def skeletons(n, total):
        skeleton = jnp.dot(rt[n], total.astype(bf16), preferred_element_type=f32)
        sbuf[n] = skeleton.reshape(2, 2, part, width)
        send(SC, n, sbuf.at[n, :, 1 - core], sgot.at[n], to_core)

    def reduce_chip(n):
        got(SC, n, sgot.at[n], to_core)
        ysend[n] = (sbuf[n, other, core] + sgot[n, other]).astype(ysend.dtype)
        send(SY, n, ysend.at[n], ygot.at[n], to_y)

    def relay(n):
        got(TY, n, tb.at[n, yp, 0], to_y)
        send(TG, n, tb.at[n, yp, 0], zb.at[n, yp, 0], to_z)
        send(TF, n, tb.at[n, yp, 0], tb.at[n, yp, 0], to_core)

    def spread(n):
        got(TZ, n, zb.at[n, c], to_z)
        send(ZC, n, zb.at[n, c], zb.at[n, c], to_core)

    def hand_on(n):
        got(TG, n, zb.at[n, yp, 0], to_z)
        send(ZG, n, zb.at[n, yp, 0], zb.at[n, yp, 0], to_core)

    def whole_transfer(n):
        got(TC, n, tb.at[n, cp], to_core)
        got(TF, n, tb.at[n, dg, 0], to_core)
        top, low = square(tb, n, 0).T, square(tb, n, 1).T
        mt[n, :, pl.ds(0, width)] = top
        mt[n, :, pl.ds(width, width)] = low
        mt[n, :, pl.ds(2 * width, width)] = top

    def couple(n):
        got(ZC, n, zb.at[n, cp], to_core)
        got(ZG, n, zb.at[n, dg, 0], to_core)
        mv[n] = times_full(kv[n], zb, n)

    def partial(n):
        xb[...] = times_full(sbuf[n].reshape(width, width), tb, n).reshape(4, part, width)
        xb[c] = xb[c] + mv[n]
        top, low = halves(xb[...].reshape(width, width))
        rhs = jnp.concatenate([top, top, low], axis=0)
        own = jnp.dot(mt[n], rhs, preferred_element_type=f32)
        pbuf[n] = own.reshape(2, 2, part, width)
        send(PC, n, pbuf.at[n, :, 1 - core], pgot.at[n], to_core)

    def parent_send(n):
        got(PC, n, pgot.at[n], to_core)
        over = (pbuf[n, other, core] + pgot[n, other]).astype(bf16)
        own = pbuf[n, y, core] + pgot[n, y]
        over_send[n] = over
        send(PD, n, over_send.at[n], din.at[n], to_d)
        own_send[n] = own.astype(bf16)
        send(PZ, n, own_send.at[n], zin.at[n], to_z)
        send(PY, n, over_send.at[n], yin.at[n], to_y)
        pv[n] = own

    outs = []

    def store(which, n, ref):
        one = pltpu.make_async_copy(ref.at[n], out_ref.at[which, n], out_sem.at[which, n])
        one.start()
        outs.append(one)

    def merge(n):
        got(SY, n, ygot.at[n], to_y)
        mine = sbuf[n, y, core] + sgot[n, y] + ygot[n].astype(f32)
        live = (row_at < ranks_ref[n]) & (col_at < ranks_ref[n])
        mv[n] = mv[n] + times_full(jnp.where(live, mine, 0.0), tb, n)
        store(0, n, mv)

    def parent_all(n):
        got(PY, n, yin.at[n], to_y)
        got(PZ, n, zin.at[n], to_z)
        got(PD, n, din.at[n], to_d)
        pv[n] = (pv[n] + yin[n].astype(f32)) + (zin[n].astype(f32) + din[n].astype(f32))
        store(1, n, pv)

    r_in.wait()
    for n in range(nodes):
        rt[n] = rv[n].T
    skeletons(0, eliminate(0, begin(0)))
    for n in range(nodes):
        relay(n)
    for n in range(nodes):
        spread(n)
    reduce_chip(0)
    for n in range(nodes):
        whole_transfer(n)
    k_in.wait()
    for n in range(1, last):
        skeletons(n, eliminate(n, begin(n)))
    total = begin(last)
    for n in range(1, last):
        reduce_chip(n)
    for n in range(nodes):
        hand_on(n)
    for n in range(nodes):
        couple(n)
    for n in range(last):
        partial(n)
    for n in range(last):
        parent_send(n)
    skeletons(last, eliminate(last, total))
    partial(last)
    reduce_chip(last)
    parent_send(last)
    for n in range(last):
        merge(n)
        parent_all(n)
    merge(last)
    parent_all(last)
    for one in sent:
        one.wait_send()
    for one in outs:
        one.wait()


def shards(diagonal_inverses, column_basis, row_basis, transfer, coupling, ranks):
    nodes, block, whole = diagonal_inverses.shape
    part, width = transfer.shape[1:]
    f32, bf16 = jnp.float32, jnp.bfloat16
    anywhere = pl.BlockSpec(memory_space=pl.ANY)
    strips = (nodes, part, width)
    quads = (nodes, 2, 2, part, width)
    pairs = (nodes, 2, part, width)
    vmem = pltpu.VMEM
    dma = pltpu.SemaphoreType.DMA
    out = pl.pallas_call(
        kernel,
        out_shape=jax.ShapeDtypeStruct((2,) + strips, f32),
        in_specs=[pl.BlockSpec(memory_space=pltpu.SMEM)] + [anywhere] * 5,
        out_specs=anywhere,
        scratch_shapes=[
            vmem((nodes, block, whole), bf16),
            vmem((nodes, whole, width), bf16),
            vmem((nodes, block, width), bf16),
            vmem(strips, f32),
            vmem(strips, f32),
            vmem((nodes, 4, 2, part, width), bf16),
            vmem((nodes, 4, 2, part, width), bf16),
            vmem((nodes, width, block), bf16),
            vmem((nodes, width, 3 * width), bf16),
            vmem((4, part, width), f32),
            vmem(quads, f32),
            vmem(pairs, f32),
            vmem(strips, bf16),
            vmem(strips, bf16),
            vmem(quads, f32),
            vmem(pairs, f32),
            vmem(strips, bf16),
            vmem(strips, bf16),
            vmem(strips, bf16),
            vmem(strips, bf16),
            vmem(strips, bf16),
            vmem(strips, f32),
            vmem(strips, f32),
            dma((KINDS, nodes)),
            dma((KINDS, nodes)),
            dma((nodes, PIECES)),
            dma((nodes, PIECES)),
            dma((nodes, PIECES)),
            dma((nodes, PIECES)),
            dma((nodes, 5)),
            dma((3,)),
            dma((2, nodes)),
        ],
        compiler_params=pltpu.CompilerParams(collective_id=0, has_side_effects=True),
    )(ranks, diagonal_inverses, column_basis, row_basis, transfer, coupling)
    return out[0], out[1]


def solution(mesh):
    placed = (P("row", "col", None),) * 5 + (P("row"),)
    return jax.shard_map(
        shards,
        mesh=mesh,
        in_specs=placed,
        out_specs=(P("row", "col", None), P("row", "col", None)),
        check_vma=False,
    )
```

```python
import jax
import jax.numpy as jnp
from jax import lax
from jax.experimental import pallas as pl
from jax.experimental.pallas import tpu as pltpu
from jax.sharding import PartitionSpec as P

BIT = 2
MESH = pl.DeviceIdType.MESH
LC, TY, TC, TF, TZ, TG, ZC, ZG, SC, SY, PC, PY, PZ, PD = range(14)
KINDS = 14
PIECES = 4


def kernel(
    ranks_ref, d_ref, l_ref, r_ref, t_ref, k_ref, out_ref,
    dv, lv, rv, tv, kv, tb, zb, rt, mt, xb, sbuf, sgot, ysend, ygot, pbuf, pgot,
    own_send, over_full, over_send, yin, zin, din, mv, pv,
    send_sem, recv_sem, ly_send, ly_recv, lf_send, lf_recv, d_sem, loc_sem, out_sem,
):
    nodes, block, _ = l_ref.shape
    part = t_ref.shape[1]
    width = t_ref.shape[2]
    f32, bf16 = jnp.float32, jnp.bfloat16
    c = lax.axis_index("col")
    r = lax.axis_index("row")
    core = lax.rem(c, 2)
    y = lax.div(c, 2)
    cp = c + 1 - 2 * core
    yp = c + 2 - 4 * y
    dg = cp + yp - c
    high = lax.rem(lax.div(r, 1 << BIT), 2)
    sib = r + (1 << BIT) - (2 << BIT) * high
    other = 1 - y
    last = nodes - 1

    to_core = {"col": cp}
    to_y = {"col": yp}
    to_z = {"row": sib}
    to_d = {"row": sib, "col": yp}
    slots = (c, cp, yp, dg)

    barrier = pltpu.get_barrier_semaphore()
    for device in (to_z, to_d, to_y, to_core):
        pl.semaphore_signal(barrier, inc=1, device_id=device, device_id_type=MESH)

    t_in = pltpu.make_async_copy(t_ref, tv, loc_sem.at[0])
    t_in.start()
    l_in, d_in = [], []
    for n in range(nodes):
        one = pltpu.make_async_copy(l_ref.at[n], lv.at[n, pl.ds(0, block)], d_sem.at[n, 4])
        one.start()
        l_in.append(one)
        for s in range(4):
            src = d_ref.at[n, :, pl.ds(pl.multiple_of(slots[s] * block, block), block)]
            one = pltpu.make_async_copy(src, dv.at[n, :, pl.ds(s * block, block)], d_sem.at[n, s])
            one.start()
            d_in.append(one)
        if n == 0:
            r_in = pltpu.make_async_copy(r_ref, rv, loc_sem.at[1])
            r_in.start()
    k_in = pltpu.make_async_copy(k_ref, kv, loc_sem.at[2])
    k_in.start()

    sent = []

    def remote(sems, src, dst, device):
        return pltpu.make_async_remote_copy(
            src_ref=src, dst_ref=dst, send_sem=sems[0], recv_sem=sems[1],
            device_id=device, device_id_type=MESH,
        )

    def of(kind, n):
        return send_sem.at[kind, n], recv_sem.at[kind, n]

    def send(kind, n, src, dst, device):
        one = remote(of(kind, n), src, dst, device)
        one.start()
        sent.append(one)

    def got(kind, n, ref, device):
        remote(of(kind, n), ref, ref, device).wait_recv()

    def halves(x):
        top = x.astype(bf16)
        return top, (x - top.astype(f32)).astype(bf16)

    def square(buf, n, level):
        return buf[n, :, level].reshape(width, width)

    def times_full(x, buf, n):
        top, low = halves(x)
        lhs = jnp.concatenate([top, low, top], axis=1)
        b_top, b_low = square(buf, n, 0), square(buf, n, 1)
        rhs = jnp.concatenate([b_top, b_top, b_low], axis=0)
        return jnp.dot(lhs, rhs, preferred_element_type=f32)

    def cuts(n):
        half, quarter = block // 2, block // 4
        if n < last:
            return ((0, half), (half, block - half))
        return ((0, half), (half, quarter), (half + quarter, block - half - quarter))

    def piece(n, s, cut):
        return lv.at[n, pl.ds(s * block + cut[0], cut[1])]

    def send_basis(n):
        for i, cut in enumerate(cuts(n)):
            one = remote(
                (ly_send.at[n, i], ly_recv.at[n, i]),
                l_ref.at[n, pl.ds(cut[0], cut[1])], piece(n, 2, cut), to_y,
            )
            one.start()
            sent.append(one)

    def send_core(n):
        send(LC, n, l_ref.at[n], lv.at[n, pl.ds(block, block)], to_core)

    row_at = lax.broadcasted_iota(jnp.int32, (part, width), 0) + c * part
    col_at = lax.broadcasted_iota(jnp.int32, (part, width), 1)
    zeros = jnp.zeros((part, width), bf16)

    pl.semaphore_wait(barrier, 4)
    send_basis(0)
    send_core(0)
    t_in.wait()
    for n in range(nodes):
        top, low = halves(jnp.where(row_at < ranks_ref[n], tv[n], 0.0))
        tb[n, c, 0] = top
        tb[n, c, 1] = low
        for buf in (tb, zb):
            for strip in (yp, dg):
                buf[n, strip, 1] = zeros
    for n in range(nodes):
        send(TZ, n, tb.at[n, c], zb.at[n, c], to_z)
        send(TY, n, tb.at[n, c, 0], tb.at[n, c, 0], to_y)
        send(TC, n, tb.at[n, c], tb.at[n, c], to_core)
    for n in range(1, nodes):
        send_basis(n)
        send_core(n)

    def times(n, first, size):
        span = pl.ds(first, size)
        return jnp.dot(dv[n, :, span], lv[n, span, :], preferred_element_type=f32)

    def begin(n):
        l_in[n].wait()
        for s in range(4):
            d_in[4 * n + s].wait()
        got(LC, n, lv.at[n, pl.ds(block, block)], to_core)
        return times(n, 0, 2 * block)

    totals = {}

    def start(n):
        totals[n] = begin(n)

    def pass_on(n, i):
        mine = piece(n, 2, cuts(n)[i])
        remote((ly_send.at[n, i], ly_recv.at[n, i]), mine, mine, to_y).wait_recv()
        one = remote((lf_send.at[n, i], lf_recv.at[n, i]), mine, piece(n, 3, cuts(n)[i]), to_core)
        one.start()
        sent.append(one)

    def far(n, i):
        cut = cuts(n)[i]
        totals[n] = totals[n] + times(n, 2 * block + cut[0], cut[1])

    def near(n, i):
        cut = cuts(n)[i]
        theirs = piece(n, 3, cut)
        remote((lf_send.at[n, i], lf_recv.at[n, i]), theirs, theirs, to_core).wait_recv()
        totals[n] = totals[n] + times(n, 3 * block + cut[0], cut[1])

    def finish(n):
        skeletons(n, totals[n])

    def right(n):
        rt[n] = rv[n].T

    def waits(n):
        r_in.wait()
        k_in.wait()

    def skeletons(n, total):
        skeleton = jnp.dot(rt[n], total.astype(bf16), preferred_element_type=f32)
        sbuf[n] = skeleton.reshape(2, 2, part, width)
        send(SC, n, sbuf.at[n, :, 1 - core], sgot.at[n], to_core)

    def reduce_chip(n):
        got(SC, n, sgot.at[n], to_core)
        ysend[n] = (sbuf[n, other, core] + sgot[n, other]).astype(ysend.dtype)
        send(SY, n, ysend.at[n], ygot.at[n], to_y)

    def relay(n):
        got(TY, n, tb.at[n, yp, 0], to_y)
        send(TG, n, tb.at[n, yp, 0], zb.at[n, yp, 0], to_z)
        send(TF, n, tb.at[n, yp, 0], tb.at[n, yp, 0], to_core)

    def spread(n):
        got(TZ, n, zb.at[n, c], to_z)
        send(ZC, n, zb.at[n, c], zb.at[n, c], to_core)

    def hand_on(n):
        got(TG, n, zb.at[n, yp, 0], to_z)
        send(ZG, n, zb.at[n, yp, 0], zb.at[n, yp, 0], to_core)

    def whole_transfer(n):
        got(TC, n, tb.at[n, cp], to_core)
        got(TF, n, tb.at[n, dg, 0], to_core)
        top, low = square(tb, n, 0).T, square(tb, n, 1).T
        mt[n, :, pl.ds(0, width)] = top
        mt[n, :, pl.ds(width, width)] = low
        mt[n, :, pl.ds(2 * width, width)] = top

    def couple(n):
        got(ZC, n, zb.at[n, cp], to_core)
        got(ZG, n, zb.at[n, dg, 0], to_core)
        mv[n] = times_full(kv[n], zb, n)

    def partial(n):
        xb[...] = times_full(sbuf[n].reshape(width, width), tb, n).reshape(4, part, width)
        xb[c] = xb[c] + mv[n]
        top, low = halves(xb[...].reshape(width, width))
        rhs = jnp.concatenate([top, top, low], axis=0)
        own = jnp.dot(mt[n], rhs, preferred_element_type=f32)
        pbuf[n] = own.reshape(2, 2, part, width)
        send(PC, n, pbuf.at[n, :, 1 - core], pgot.at[n], to_core)

    def parent_send(n):
        got(PC, n, pgot.at[n], to_core)
        over = pbuf[n, other, core] + pgot[n, other]
        own = pbuf[n, y, core] + pgot[n, y]
        over_full[n] = over
        over_send[n] = over.astype(bf16)
        send(PD, n, over_send.at[n], din.at[n], to_d)
        own_send[n] = own.astype(bf16)
        send(PZ, n, own_send.at[n], zin.at[n], to_z)
        send(PY, n, over_full.at[n], yin.at[n], to_y)
        pv[n] = own

    outs = []

    def store(which, n, ref):
        one = pltpu.make_async_copy(ref.at[n], out_ref.at[which, n], out_sem.at[which, n])
        one.start()
        outs.append(one)

    def merge(n):
        got(SY, n, ygot.at[n], to_y)
        mine = sbuf[n, y, core] + sgot[n, y] + ygot[n].astype(f32)
        live = (row_at < ranks_ref[n]) & (col_at < ranks_ref[n])
        mv[n] = mv[n] + times_full(jnp.where(live, mine, 0.0), tb, n)
        store(0, n, mv)

    def parent_all(n):
        got(PY, n, yin.at[n], to_y)
        got(PZ, n, zin.at[n], to_z)
        got(PD, n, din.at[n], to_d)
        pv[n] = (pv[n] + yin[n]) + (zin[n].astype(f32) + din[n].astype(f32))
        store(1, n, pv)

    start(0)
    waits(0)
    right(0)
    right(1)
    right(2)
    start(1)
    start(2)
    pass_on(0, 0)
    far(0, 0)
    near(0, 0)
    pass_on(0, 1)
    far(0, 1)
    near(0, 1)
    finish(0)
    relay(0)
    relay(1)
    relay(2)
    spread(0)
    spread(1)
    spread(2)
    reduce_chip(0)
    whole_transfer(0)
    whole_transfer(1)
    whole_transfer(2)
    pass_on(1, 0)
    far(1, 0)
    near(1, 0)
    pass_on(1, 1)
    far(1, 1)
    hand_on(0)
    hand_on(1)
    hand_on(2)
    near(1, 1)
    finish(1)
    couple(0)
    partial(0)
    couple(1)
    partial(1)
    reduce_chip(1)
    pass_on(2, 0)
    far(2, 0)
    couple(2)
    near(2, 0)
    parent_send(0)
    pass_on(2, 1)
    far(2, 1)
    parent_send(1)
    near(2, 1)
    pass_on(2, 2)
    far(2, 2)
    near(2, 2)
    finish(2)
    partial(2)
    reduce_chip(2)
    parent_send(2)
    merge(0)
    merge(1)
    parent_all(0)
    parent_all(1)
    merge(2)
    parent_all(2)
    for one in sent:
        one.wait_send()
    for one in outs:
        one.wait()


def shards(diagonal_inverses, column_basis, row_basis, transfer, coupling, ranks):
    nodes, block, whole = diagonal_inverses.shape
    part, width = transfer.shape[1:]
    f32, bf16 = jnp.float32, jnp.bfloat16
    anywhere = pl.BlockSpec(memory_space=pl.ANY)
    strips = (nodes, part, width)
    quads = (nodes, 2, 2, part, width)
    pairs = (nodes, 2, part, width)
    vmem = pltpu.VMEM
    dma = pltpu.SemaphoreType.DMA
    out = pl.pallas_call(
        kernel,
        out_shape=jax.ShapeDtypeStruct((2,) + strips, f32),
        in_specs=[pl.BlockSpec(memory_space=pltpu.SMEM)] + [anywhere] * 5,
        out_specs=anywhere,
        scratch_shapes=[
            vmem((nodes, block, whole), bf16),
            vmem((nodes, whole, width), bf16),
            vmem((nodes, block, width), bf16),
            vmem(strips, f32),
            vmem(strips, f32),
            vmem((nodes, 4, 2, part, width), bf16),
            vmem((nodes, 4, 2, part, width), bf16),
            vmem((nodes, width, block), bf16),
            vmem((nodes, width, 3 * width), bf16),
            vmem((4, part, width), f32),
            vmem(quads, f32),
            vmem(pairs, f32),
            vmem(strips, bf16),
            vmem(strips, bf16),
            vmem(quads, f32),
            vmem(pairs, f32),
            vmem(strips, bf16),
            vmem(strips, f32),
            vmem(strips, bf16),
            vmem(strips, f32),
            vmem(strips, bf16),
            vmem(strips, bf16),
            vmem(strips, f32),
            vmem(strips, f32),
            dma((KINDS, nodes)),
            dma((KINDS, nodes)),
            dma((nodes, PIECES)),
            dma((nodes, PIECES)),
            dma((nodes, PIECES)),
            dma((nodes, PIECES)),
            dma((nodes, 5)),
            dma((3,)),
            dma((2, nodes)),
        ],
        compiler_params=pltpu.CompilerParams(collective_id=0, has_side_effects=True),
    )(ranks, diagonal_inverses, column_basis, row_basis, transfer, coupling)
    return out[0], out[1]


def solution(mesh):
    placed = (P("row", "col", None),) * 5 + (P("row"),)
    return jax.shard_map(
        shards,
        mesh=mesh,
        in_specs=placed,
        out_specs=(P("row", "col", None), P("row", "col", None)),
        check_vma=False,
    )
```

```python
import jax
import jax.numpy as jnp
from jax import lax
from jax.experimental import pallas as pl
from jax.experimental.pallas import tpu as pltpu
from jax.sharding import PartitionSpec as P

BIT = 2
MESH = pl.DeviceIdType.MESH
LC, TY, TC, TF, TZ, TG, ZC, ZG, SC, SY, PC, PY, PZ, PD = range(14)
KINDS = 14
PIECES = 4


def kernel(
    ranks_ref, d_ref, l_ref, r_ref, t_ref, k_ref, out_ref,
    dv, lv, rv, tv, kv, tb, zb, rt, mt, xb, sbuf, sgot, ysend, ygot, pbuf, pgot,
    own_send, over_full, over_send, yin, zin, din, mv, pv,
    send_sem, recv_sem, ly_send, ly_recv, lf_send, lf_recv, d_sem, loc_sem, out_sem,
):
    nodes, block, _ = l_ref.shape
    part = t_ref.shape[1]
    width = t_ref.shape[2]
    f32, bf16 = jnp.float32, jnp.bfloat16
    c = lax.axis_index("col")
    r = lax.axis_index("row")
    core = lax.rem(c, 2)
    y = lax.div(c, 2)
    cp = c + 1 - 2 * core
    yp = c + 2 - 4 * y
    dg = cp + yp - c
    high = lax.rem(lax.div(r, 1 << BIT), 2)
    sib = r + (1 << BIT) - (2 << BIT) * high
    other = 1 - y
    last = nodes - 1

    to_core = {"col": cp}
    to_y = {"col": yp}
    to_z = {"row": sib}
    to_d = {"row": sib, "col": yp}
    slots = (c, cp, yp, dg)

    barrier = pltpu.get_barrier_semaphore()
    for device in (to_z, to_d, to_y, to_core):
        pl.semaphore_signal(barrier, inc=1, device_id=device, device_id_type=MESH)

    t_in = pltpu.make_async_copy(t_ref, tv, loc_sem.at[0])
    t_in.start()
    l_in, d_in = [], []

    def load(n):
        one = pltpu.make_async_copy(l_ref.at[n], lv.at[n, pl.ds(0, block)], d_sem.at[n, 4])
        one.start()
        l_in.append(one)
        for s in range(4):
            src = d_ref.at[n, :, pl.ds(pl.multiple_of(slots[s] * block, block), block)]
            one = pltpu.make_async_copy(src, dv.at[n, :, pl.ds(s * block, block)], d_sem.at[n, s])
            one.start()
            d_in.append(one)

    load(0)
    r_in = pltpu.make_async_copy(r_ref, rv, loc_sem.at[1])
    r_in.start()
    k_in = pltpu.make_async_copy(k_ref, kv, loc_sem.at[2])
    k_in.start()
    sent = []

    def remote(sems, src, dst, device):
        return pltpu.make_async_remote_copy(
            src_ref=src, dst_ref=dst, send_sem=sems[0], recv_sem=sems[1],
            device_id=device, device_id_type=MESH,
        )

    def of(kind, n):
        return send_sem.at[kind, n], recv_sem.at[kind, n]

    def send(kind, n, src, dst, device):
        one = remote(of(kind, n), src, dst, device)
        one.start()
        sent.append(one)

    def got(kind, n, ref, device):
        remote(of(kind, n), ref, ref, device).wait_recv()

    def halves(x):
        top = x.astype(bf16)
        return top, (x - top.astype(f32)).astype(bf16)

    def square(buf, n, level):
        return buf[n, :, level].reshape(width, width)

    def times_full(x, buf, n):
        top, low = halves(x)
        lhs = jnp.concatenate([top, low, top], axis=1)
        b_top, b_low = square(buf, n, 0), square(buf, n, 1)
        rhs = jnp.concatenate([b_top, b_top, b_low], axis=0)
        return jnp.dot(lhs, rhs, preferred_element_type=f32)

    def cuts(n):
        half, quarter = block // 2, block // 4
        if n < last:
            return ((0, half), (half, block - half))
        return ((0, half), (half, quarter), (half + quarter, block - half - quarter))

    def piece(n, s, cut):
        return lv.at[n, pl.ds(s * block + cut[0], cut[1])]

    def send_basis(n):
        for i, cut in enumerate(cuts(n)):
            one = remote(
                (ly_send.at[n, i], ly_recv.at[n, i]),
                l_ref.at[n, pl.ds(cut[0], cut[1])], piece(n, 2, cut), to_y,
            )
            one.start()
            sent.append(one)

    def send_core(n):
        send(LC, n, l_ref.at[n], lv.at[n, pl.ds(block, block)], to_core)

    row_at = lax.broadcasted_iota(jnp.int32, (part, width), 0) + c * part
    col_at = lax.broadcasted_iota(jnp.int32, (part, width), 1)
    zeros = jnp.zeros((part, width), bf16)

    pl.semaphore_wait(barrier, 4)
    send_basis(0)
    send_core(0)
    t_in.wait()
    for n in range(nodes):
        top, low = halves(jnp.where(row_at < ranks_ref[n], tv[n], 0.0))
        tb[n, c, 0] = top
        tb[n, c, 1] = low
        for buf in (tb, zb):
            for strip in (yp, dg):
                buf[n, strip, 1] = zeros
    for n in range(nodes):
        send(TZ, n, tb.at[n, c], zb.at[n, c], to_z)
        send(TY, n, tb.at[n, c, 0], tb.at[n, c, 0], to_y)
        send(TC, n, tb.at[n, c], tb.at[n, c], to_core)
    for n in range(1, nodes):
        send_basis(n)
        send_core(n)

    for n in range(1, nodes):
        load(n)

    def times(n, first, size):
        span = pl.ds(first, size)
        return jnp.dot(dv[n, :, span], lv[n, span, :], preferred_element_type=f32)

    def begin(n):
        l_in[n].wait()
        for s in range(4):
            d_in[4 * n + s].wait()
        got(LC, n, lv.at[n, pl.ds(block, block)], to_core)
        return times(n, 0, 2 * block)

    totals = {}

    def start(n):
        totals[n] = begin(n)

    def pass_on(n, i):
        mine = piece(n, 2, cuts(n)[i])
        remote((ly_send.at[n, i], ly_recv.at[n, i]), mine, mine, to_y).wait_recv()
        one = remote((lf_send.at[n, i], lf_recv.at[n, i]), mine, piece(n, 3, cuts(n)[i]), to_core)
        one.start()
        sent.append(one)

    def far(n, i):
        cut = cuts(n)[i]
        totals[n] = totals[n] + times(n, 2 * block + cut[0], cut[1])

    def near(n, i):
        cut = cuts(n)[i]
        theirs = piece(n, 3, cut)
        remote((lf_send.at[n, i], lf_recv.at[n, i]), theirs, theirs, to_core).wait_recv()
        totals[n] = totals[n] + times(n, 3 * block + cut[0], cut[1])

    def finish(n):
        skeletons(n, totals[n])

    def right(n):
        rt[n] = rv[n].T

    def waits(n):
        r_in.wait()
        k_in.wait()

    def skeletons(n, total):
        skeleton = jnp.dot(rt[n], total.astype(bf16), preferred_element_type=f32)
        sbuf[n] = skeleton.reshape(2, 2, part, width)
        send(SC, n, sbuf.at[n, :, 1 - core], sgot.at[n], to_core)

    def reduce_chip(n):
        got(SC, n, sgot.at[n], to_core)
        ysend[n] = (sbuf[n, other, core] + sgot[n, other]).astype(ysend.dtype)
        send(SY, n, ysend.at[n], ygot.at[n], to_y)

    def relay(n):
        got(TY, n, tb.at[n, yp, 0], to_y)
        send(TG, n, tb.at[n, yp, 0], zb.at[n, yp, 0], to_z)
        send(TF, n, tb.at[n, yp, 0], tb.at[n, yp, 0], to_core)

    def spread(n):
        got(TZ, n, zb.at[n, c], to_z)
        send(ZC, n, zb.at[n, c], zb.at[n, c], to_core)

    def hand_on(n):
        got(TG, n, zb.at[n, yp, 0], to_z)
        send(ZG, n, zb.at[n, yp, 0], zb.at[n, yp, 0], to_core)

    def whole_transfer(n):
        got(TC, n, tb.at[n, cp], to_core)
        got(TF, n, tb.at[n, dg, 0], to_core)
        top, low = square(tb, n, 0).T, square(tb, n, 1).T
        mt[n, :, pl.ds(0, width)] = top
        mt[n, :, pl.ds(width, width)] = low
        mt[n, :, pl.ds(2 * width, width)] = top

    def couple(n):
        got(ZC, n, zb.at[n, cp], to_core)
        got(ZG, n, zb.at[n, dg, 0], to_core)
        mv[n] = times_full(kv[n], zb, n)

    def partial(n):
        xb[...] = times_full(sbuf[n].reshape(width, width), tb, n).reshape(4, part, width)
        xb[c] = xb[c] + mv[n]
        top, low = halves(xb[...].reshape(width, width))
        rhs = jnp.concatenate([top, top, low], axis=0)
        own = jnp.dot(mt[n], rhs, preferred_element_type=f32)
        pbuf[n] = own.reshape(2, 2, part, width)
        send(PC, n, pbuf.at[n, :, 1 - core], pgot.at[n], to_core)

    def parent_send(n):
        got(PC, n, pgot.at[n], to_core)
        over = pbuf[n, other, core] + pgot[n, other]
        own = pbuf[n, y, core] + pgot[n, y]
        over_full[n] = over
        over_send[n] = over.astype(bf16)
        send(PD, n, over_send.at[n], din.at[n], to_d)
        own_send[n] = own.astype(bf16)
        send(PZ, n, own_send.at[n], zin.at[n], to_z)
        send(PY, n, over_full.at[n], yin.at[n], to_y)
        pv[n] = own

    outs = []

    def store(which, n, ref):
        one = pltpu.make_async_copy(ref.at[n], out_ref.at[which, n], out_sem.at[which, n])
        one.start()
        outs.append(one)

    def merge(n):
        got(SY, n, ygot.at[n], to_y)
        mine = sbuf[n, y, core] + sgot[n, y] + ygot[n].astype(f32)
        live = (row_at < ranks_ref[n]) & (col_at < ranks_ref[n])
        mv[n] = mv[n] + times_full(jnp.where(live, mine, 0.0), tb, n)
        store(0, n, mv)

    def parent_all(n):
        got(PY, n, yin.at[n], to_y)
        got(PZ, n, zin.at[n], to_z)
        got(PD, n, din.at[n], to_d)
        pv[n] = (pv[n] + yin[n]) + (zin[n].astype(f32) + din[n].astype(f32))
        store(1, n, pv)

    start(0)
    waits(0)
    right(0)
    right(1)
    right(2)
    start(1)
    start(2)
    pass_on(0, 0)
    far(0, 0)
    near(0, 0)
    pass_on(0, 1)
    far(0, 1)
    near(0, 1)
    finish(0)
    relay(0)
    relay(1)
    relay(2)
    spread(0)
    spread(1)
    spread(2)
    reduce_chip(0)
    whole_transfer(0)
    whole_transfer(1)
    whole_transfer(2)
    pass_on(1, 0)
    far(1, 0)
    near(1, 0)
    pass_on(1, 1)
    far(1, 1)
    hand_on(0)
    hand_on(1)
    hand_on(2)
    near(1, 1)
    finish(1)
    couple(0)
    partial(0)
    couple(1)
    partial(1)
    parent_send(0)
    reduce_chip(1)
    pass_on(2, 0)
    parent_send(1)
    far(2, 0)
    couple(2)
    near(2, 0)
    pass_on(2, 1)
    far(2, 1)
    near(2, 1)
    pass_on(2, 2)
    far(2, 2)
    near(2, 2)
    finish(2)
    partial(2)
    reduce_chip(2)
    parent_send(2)
    merge(0)
    merge(1)
    parent_all(0)
    parent_all(1)
    merge(2)
    parent_all(2)
    for one in sent:
        one.wait_send()
    for one in outs:
        one.wait()


def shards(diagonal_inverses, column_basis, row_basis, transfer, coupling, ranks):
    nodes, block, whole = diagonal_inverses.shape
    part, width = transfer.shape[1:]
    f32, bf16 = jnp.float32, jnp.bfloat16
    anywhere = pl.BlockSpec(memory_space=pl.ANY)
    strips = (nodes, part, width)
    quads = (nodes, 2, 2, part, width)
    pairs = (nodes, 2, part, width)
    vmem = pltpu.VMEM
    dma = pltpu.SemaphoreType.DMA
    out = pl.pallas_call(
        kernel,
        out_shape=jax.ShapeDtypeStruct((2,) + strips, f32),
        in_specs=[pl.BlockSpec(memory_space=pltpu.SMEM)] + [anywhere] * 5,
        out_specs=anywhere,
        scratch_shapes=[
            vmem((nodes, block, whole), bf16),
            vmem((nodes, whole, width), bf16),
            vmem((nodes, block, width), bf16),
            vmem(strips, f32),
            vmem(strips, f32),
            vmem((nodes, 4, 2, part, width), bf16),
            vmem((nodes, 4, 2, part, width), bf16),
            vmem((nodes, width, block), bf16),
            vmem((nodes, width, 3 * width), bf16),
            vmem((4, part, width), f32),
            vmem(quads, f32),
            vmem(pairs, f32),
            vmem(strips, bf16),
            vmem(strips, bf16),
            vmem(quads, f32),
            vmem(pairs, f32),
            vmem(strips, bf16),
            vmem(strips, f32),
            vmem(strips, bf16),
            vmem(strips, f32),
            vmem(strips, bf16),
            vmem(strips, bf16),
            vmem(strips, f32),
            vmem(strips, f32),
            dma((KINDS, nodes)),
            dma((KINDS, nodes)),
            dma((nodes, PIECES)),
            dma((nodes, PIECES)),
            dma((nodes, PIECES)),
            dma((nodes, PIECES)),
            dma((nodes, 5)),
            dma((3,)),
            dma((2, nodes)),
        ],
        compiler_params=pltpu.CompilerParams(collective_id=0, has_side_effects=True),
    )(ranks, diagonal_inverses, column_basis, row_basis, transfer, coupling)
    return out[0], out[1]


def solution(mesh):
    placed = (P("row", "col", None),) * 5 + (P("row"),)
    return jax.shard_map(
        shards,
        mesh=mesh,
        in_specs=placed,
        out_specs=(P("row", "col", None), P("row", "col", None)),
        check_vma=False,
    )
```

```python
import jax
import jax.numpy as jnp
from jax import lax
from jax.experimental import pallas as pl
from jax.experimental.pallas import tpu as pltpu
from jax.sharding import PartitionSpec as P

BIT = 2
MESH = pl.DeviceIdType.MESH
LC, TY, TC, TF, TZ, TG, ZC, ZG, SC, SY, PC, PY, PZ, PD = range(14)
KINDS = 14
PIECES = 4


def kernel(
    ranks_ref, d_ref, l_ref, r_ref, t_ref, k_ref, out_ref,
    dv, lv, rv, tv, kv, tb, zb, rt, mt, xb, sbuf, sgot, ysend, ygot, pbuf, pgot,
    own_send, over_full, over_send, yin, zin, din, mv, pv,
    send_sem, recv_sem, ly_send, ly_recv, lf_send, lf_recv, d_sem, loc_sem, out_sem,
):
    nodes, block, _ = l_ref.shape
    part = t_ref.shape[1]
    width = t_ref.shape[2]
    f32, bf16 = jnp.float32, jnp.bfloat16
    c = lax.axis_index("col")
    r = lax.axis_index("row")
    core = lax.rem(c, 2)
    y = lax.div(c, 2)
    cp = c + 1 - 2 * core
    yp = c + 2 - 4 * y
    dg = cp + yp - c
    high = lax.rem(lax.div(r, 1 << BIT), 2)
    sib = r + (1 << BIT) - (2 << BIT) * high
    other = 1 - y
    last = nodes - 1

    to_core = {"col": cp}
    to_y = {"col": yp}
    to_z = {"row": sib}
    to_d = {"row": sib, "col": yp}
    slots = (c, cp, yp, dg)

    barrier = pltpu.get_barrier_semaphore()
    for device in (to_z, to_d, to_y, to_core):
        pl.semaphore_signal(barrier, inc=1, device_id=device, device_id_type=MESH)

    t_in = pltpu.make_async_copy(t_ref, tv, loc_sem.at[0])
    t_in.start()
    l_in, d_in = [], []

    def load(n):
        one = pltpu.make_async_copy(l_ref.at[n], lv.at[n, pl.ds(0, block)], d_sem.at[n, 4])
        one.start()
        l_in.append(one)
        for s in range(4):
            src = d_ref.at[n, :, pl.ds(pl.multiple_of(slots[s] * block, block), block)]
            one = pltpu.make_async_copy(src, dv.at[n, :, pl.ds(s * block, block)], d_sem.at[n, s])
            one.start()
            d_in.append(one)

    load(0)
    r_in = pltpu.make_async_copy(r_ref, rv, loc_sem.at[1])
    r_in.start()
    k_in = pltpu.make_async_copy(k_ref, kv, loc_sem.at[2])
    k_in.start()
    sent = []

    def remote(sems, src, dst, device):
        return pltpu.make_async_remote_copy(
            src_ref=src, dst_ref=dst, send_sem=sems[0], recv_sem=sems[1],
            device_id=device, device_id_type=MESH,
        )

    def of(kind, n):
        return send_sem.at[kind, n], recv_sem.at[kind, n]

    def send(kind, n, src, dst, device):
        one = remote(of(kind, n), src, dst, device)
        one.start()
        sent.append(one)

    def got(kind, n, ref, device):
        remote(of(kind, n), ref, ref, device).wait_recv()

    def halves(x):
        top = x.astype(bf16)
        return top, (x - top.astype(f32)).astype(bf16)

    def square(buf, n, level):
        return buf[n, :, level].reshape(width, width)

    def times_full(x, buf, n):
        top, low = halves(x)
        lhs = jnp.concatenate([top, low, top], axis=1)
        b_top, b_low = square(buf, n, 0), square(buf, n, 1)
        rhs = jnp.concatenate([b_top, b_top, b_low], axis=0)
        return jnp.dot(lhs, rhs, preferred_element_type=f32)

    def cuts(n):
        half, quarter = block // 2, block // 4
        if n < last:
            return ((0, half), (half, block - half))
        return ((0, half), (half, quarter), (half + quarter, block - half - quarter))

    def piece(n, s, cut):
        return lv.at[n, pl.ds(s * block + cut[0], cut[1])]

    def send_basis(n):
        for i, cut in enumerate(cuts(n)):
            one = remote(
                (ly_send.at[n, i], ly_recv.at[n, i]),
                l_ref.at[n, pl.ds(cut[0], cut[1])], piece(n, 2, cut), to_y,
            )
            one.start()
            sent.append(one)

    def send_core(n):
        send(LC, n, l_ref.at[n], lv.at[n, pl.ds(block, block)], to_core)

    row_at = lax.broadcasted_iota(jnp.int32, (part, width), 0) + c * part
    col_at = lax.broadcasted_iota(jnp.int32, (part, width), 1)
    zeros = jnp.zeros((part, width), bf16)

    pl.semaphore_wait(barrier, 4)
    send_basis(0)
    send_core(0)
    t_in.wait()
    for n in range(nodes):
        top, low = halves(jnp.where(row_at < ranks_ref[n], tv[n], 0.0))
        tb[n, c, 0] = top
        tb[n, c, 1] = low
        for buf in (tb, zb):
            for strip in (yp, dg):
                buf[n, strip, 1] = zeros
    for n in range(nodes):
        send(TZ, n, tb.at[n, c], zb.at[n, c], to_z)
        send(TY, n, tb.at[n, c, 0], tb.at[n, c, 0], to_y)
        send(TC, n, tb.at[n, c], tb.at[n, c], to_core)
    for n in range(1, nodes):
        send_basis(n)
        send_core(n)

    for n in range(1, nodes):
        load(n)

    def times(n, first, size):
        span = pl.ds(first, size)
        return jnp.dot(dv[n, :, span], lv[n, span, :], preferred_element_type=f32)

    def begin(n):
        l_in[n].wait()
        for s in range(4):
            d_in[4 * n + s].wait()
        got(LC, n, lv.at[n, pl.ds(block, block)], to_core)
        return times(n, 0, 2 * block)

    totals = {}

    def start(n):
        totals[n] = begin(n)

    def pass_on(n, i):
        mine = piece(n, 2, cuts(n)[i])
        remote((ly_send.at[n, i], ly_recv.at[n, i]), mine, mine, to_y).wait_recv()
        one = remote((lf_send.at[n, i], lf_recv.at[n, i]), mine, piece(n, 3, cuts(n)[i]), to_core)
        one.start()
        sent.append(one)

    def far(n, i):
        cut = cuts(n)[i]
        totals[n] = totals[n] + times(n, 2 * block + cut[0], cut[1])

    def near(n, i):
        cut = cuts(n)[i]
        theirs = piece(n, 3, cut)
        remote((lf_send.at[n, i], lf_recv.at[n, i]), theirs, theirs, to_core).wait_recv()
        totals[n] = totals[n] + times(n, 3 * block + cut[0], cut[1])

    def finish(n):
        skeletons(n, totals[n])

    def right(n):
        rt[n] = rv[n].T

    def waits(n):
        r_in.wait()
        k_in.wait()

    def skeletons(n, total):
        skeleton = jnp.dot(rt[n], total.astype(bf16), preferred_element_type=f32)
        sbuf[n] = skeleton.reshape(2, 2, part, width)
        send(SC, n, sbuf.at[n, :, 1 - core], sgot.at[n], to_core)

    def reduce_chip(n):
        got(SC, n, sgot.at[n], to_core)
        ysend[n] = (sbuf[n, other, core] + sgot[n, other]).astype(ysend.dtype)
        send(SY, n, ysend.at[n], ygot.at[n], to_y)

    def relay(n):
        got(TY, n, tb.at[n, yp, 0], to_y)
        send(TG, n, tb.at[n, yp, 0], zb.at[n, yp, 0], to_z)
        send(TF, n, tb.at[n, yp, 0], tb.at[n, yp, 0], to_core)

    def spread(n):
        got(TZ, n, zb.at[n, c], to_z)
        send(ZC, n, zb.at[n, c], zb.at[n, c], to_core)

    def hand_on(n):
        got(TG, n, zb.at[n, yp, 0], to_z)
        send(ZG, n, zb.at[n, yp, 0], zb.at[n, yp, 0], to_core)

    def whole_transfer(n):
        got(TC, n, tb.at[n, cp], to_core)
        got(TF, n, tb.at[n, dg, 0], to_core)
        top, low = square(tb, n, 0).T, square(tb, n, 1).T
        mt[n, :, pl.ds(0, width)] = top
        mt[n, :, pl.ds(width, width)] = low
        mt[n, :, pl.ds(2 * width, width)] = top

    def couple(n):
        got(ZC, n, zb.at[n, cp], to_core)
        got(ZG, n, zb.at[n, dg, 0], to_core)
        mv[n] = times_full(kv[n], zb, n)

    def partial(n):
        xb[...] = times_full(sbuf[n].reshape(width, width), tb, n).reshape(4, part, width)
        xb[c] = xb[c] + mv[n]
        top, low = halves(xb[...].reshape(width, width))
        rhs = jnp.concatenate([top, top, low], axis=0)
        for side in (1 - core, core):
            lhs = jnp.concatenate(
                [mt[n, pl.ds(pl.multiple_of((2 * half + side) * part, part), part)] for half in range(2)], axis=0
            )
            rows = jnp.dot(lhs, rhs, preferred_element_type=f32)
            pbuf[n, :, side] = rows.reshape(2, part, width)
            if side is not core:
                send(PC, n, pbuf.at[n, :, 1 - core], pgot.at[n], to_core)

    def parent_send(n):
        got(PC, n, pgot.at[n], to_core)
        over = pbuf[n, other, core] + pgot[n, other]
        own = pbuf[n, y, core] + pgot[n, y]
        over_full[n] = over
        over_send[n] = over.astype(bf16)
        send(PD, n, over_send.at[n], din.at[n], to_d)
        own_send[n] = own.astype(bf16)
        send(PZ, n, own_send.at[n], zin.at[n], to_z)
        send(PY, n, over_full.at[n], yin.at[n], to_y)
        pv[n] = own

    outs = []

    def store(which, n, ref):
        one = pltpu.make_async_copy(ref.at[n], out_ref.at[which, n], out_sem.at[which, n])
        one.start()
        outs.append(one)

    def merge(n):
        got(SY, n, ygot.at[n], to_y)
        mine = sbuf[n, y, core] + sgot[n, y] + ygot[n].astype(f32)
        live = (row_at < ranks_ref[n]) & (col_at < ranks_ref[n])
        mv[n] = mv[n] + times_full(jnp.where(live, mine, 0.0), tb, n)
        store(0, n, mv)

    def parent_all(n):
        got(PY, n, yin.at[n], to_y)
        got(PZ, n, zin.at[n], to_z)
        got(PD, n, din.at[n], to_d)
        pv[n] = (pv[n] + yin[n]) + (zin[n].astype(f32) + din[n].astype(f32))
        store(1, n, pv)

    start(0)
    waits(0)
    right(0)
    right(1)
    right(2)
    start(1)
    start(2)
    pass_on(0, 0)
    far(0, 0)
    near(0, 0)
    pass_on(0, 1)
    far(0, 1)
    near(0, 1)
    finish(0)
    relay(0)
    relay(1)
    relay(2)
    spread(0)
    spread(1)
    spread(2)
    reduce_chip(0)
    whole_transfer(0)
    whole_transfer(1)
    whole_transfer(2)
    pass_on(1, 0)
    far(1, 0)
    near(1, 0)
    hand_on(0)
    hand_on(1)
    couple(0)
    partial(0)
    pass_on(1, 1)
    far(1, 1)
    parent_send(0)
    hand_on(2)
    couple(1)
    near(1, 1)
    finish(1)
    partial(1)
    couple(2)
    reduce_chip(1)
    parent_send(1)
    pass_on(2, 0)
    far(2, 0)
    near(2, 0)
    pass_on(2, 1)
    far(2, 1)
    near(2, 1)
    pass_on(2, 2)
    far(2, 2)
    near(2, 2)
    finish(2)
    partial(2)
    reduce_chip(2)
    parent_send(2)
    merge(0)
    merge(1)
    parent_all(0)
    parent_all(1)
    merge(2)
    parent_all(2)
    for one in sent:
        one.wait_send()
    for one in outs:
        one.wait()


def shards(diagonal_inverses, column_basis, row_basis, transfer, coupling, ranks):
    nodes, block, whole = diagonal_inverses.shape
    part, width = transfer.shape[1:]
    f32, bf16 = jnp.float32, jnp.bfloat16
    anywhere = pl.BlockSpec(memory_space=pl.ANY)
    strips = (nodes, part, width)
    quads = (nodes, 2, 2, part, width)
    pairs = (nodes, 2, part, width)
    vmem = pltpu.VMEM
    dma = pltpu.SemaphoreType.DMA
    out = pl.pallas_call(
        kernel,
        out_shape=jax.ShapeDtypeStruct((2,) + strips, f32),
        in_specs=[pl.BlockSpec(memory_space=pltpu.SMEM)] + [anywhere] * 5,
        out_specs=anywhere,
        scratch_shapes=[
            vmem((nodes, block, whole), bf16),
            vmem((nodes, whole, width), bf16),
            vmem((nodes, block, width), bf16),
            vmem(strips, f32),
            vmem(strips, f32),
            vmem((nodes, 4, 2, part, width), bf16),
            vmem((nodes, 4, 2, part, width), bf16),
            vmem((nodes, width, block), bf16),
            vmem((nodes, width, 3 * width), bf16),
            vmem((4, part, width), f32),
            vmem(quads, f32),
            vmem(pairs, f32),
            vmem(strips, bf16),
            vmem(strips, bf16),
            vmem(quads, f32),
            vmem(pairs, f32),
            vmem(strips, bf16),
            vmem(strips, f32),
            vmem(strips, bf16),
            vmem(strips, f32),
            vmem(strips, bf16),
            vmem(strips, bf16),
            vmem(strips, f32),
            vmem(strips, f32),
            dma((KINDS, nodes)),
            dma((KINDS, nodes)),
            dma((nodes, PIECES)),
            dma((nodes, PIECES)),
            dma((nodes, PIECES)),
            dma((nodes, PIECES)),
            dma((nodes, 5)),
            dma((3,)),
            dma((2, nodes)),
        ],
        compiler_params=pltpu.CompilerParams(collective_id=0, has_side_effects=True),
    )(ranks, diagonal_inverses, column_basis, row_basis, transfer, coupling)
    return out[0], out[1]


def solution(mesh):
    placed = (P("row", "col", None),) * 5 + (P("row"),)
    return jax.shard_map(
        shards,
        mesh=mesh,
        in_specs=placed,
        out_specs=(P("row", "col", None), P("row", "col", None)),
        check_vma=False,
    )
```
